32 devices in a mesh: groups: 2 (over y), dp: 4 (over z), landmark: 4 (over x, core).
Axes of the slice: x: 2, y: 2, z: 4, core: 2. Of those that a mesh axis runs over, the one named last changes fastest.
Arguments:
- images: bfloat16 [256, 1024], P(('groups', 'dp')), parts along dimension 0, may hold values from -6 to 6, as said below
- captions: bfloat16 [256, 768], P(('groups', 'dp')), parts along dimension 0, may hold values from -6 to 6, as said below
- caption_of: int32 [256], P(('groups', 'dp')), parts along dimension 0, may hold values from 0 to 31, as said below
- image_landmarks: bfloat16 [16384, 1024], P(('landmark', 'dp')), may hold values from -6 to 6
- image_gamma: float32 [16384], P(('landmark', 'dp')), may hold values from 8 to 40
- text_landmarks: bfloat16 [4096, 768], P(('dp', 'landmark')), may hold values from -6 to 6
- text_gamma: float32 [4096], P(('dp', 'landmark')), may hold values from 8 to 40
Outputs:
- zstat: float32 [32768, 4096], P(('groups', 'landmark'), 'dp'), parts along dimension 0
- image_mean: float32 [32768], P(('groups', 'landmark', 'dp')), parts along dimension 0
- text_mean: float32 [8192], P(('groups', 'dp', 'landmark')), parts along dimension 0
The draws below stay inside these ranges and needn't reach their ends.
There are 2 independent parts, one for each index of `groups`. The reference program is written for one: setup_inputs(seed, part) draws one part's arguments, and reference() takes and returns one part's arrays. A program takes and returns all parts, laid end to end along the dimension named above; an argument that names none is the same for every part. Nothing has to cross between parts.
Inputs may be any that keep to these rules, and one draw needn't show every extreme that they name: `caption_of`: within each aligned block of 32 rows (the pairs of one index of dp) the values are a permutation of 0 to 31. `images`: image rows are embeddings; no row is zero. `captions`: caption rows are embeddings; no row is zero.
All inputs are finite; a program needn't handle non-finite values.
Results may differ from the reference program's by a relative error of at most 0.03.
Values may be sent and summed in bfloat16 or wider, within the bound.
A program may use at most 128 MiB of HBM per device.

```python
import math
import jax
import jax.numpy as jnp
from jax import lax

D_IMG = 1024
D_TXT = 768
IMG_LM = 16384
TXT_LM = 4096
BLOCK = 32
PAIRS = 128


def paired_draw(key):
    shared = jax.random.normal(jax.random.fold_in(key, 11), (PAIRS, D_IMG), jnp.float32)
    noise = jax.random.normal(jax.random.fold_in(key, 12), (PAIRS, D_TXT), jnp.float32)
    return (jnp.clip(shared, -6.0, 6.0), jnp.clip(noise, -6.0, 6.0))


def pair_order(key):
    block_keys = jax.random.split(jax.random.fold_in(key, 13), PAIRS // BLOCK)
    orders = jax.vmap(lambda single: jax.random.permutation(single, BLOCK))(block_keys)
    return orders.reshape(PAIRS).astype(jnp.int32)


def draw_images(key, part):
    shared, noise = paired_draw(key)
    return shared.astype(jnp.bfloat16)


def draw_captions(key, part):
    shared, noise = paired_draw(key)
    order = pair_order(key)
    values = jnp.clip(0.8 * shared[:, :D_TXT] + 0.6 * noise, -6.0, 6.0)
    target = jnp.arange(PAIRS, dtype=jnp.int32) // BLOCK * BLOCK + order
    placed = jnp.zeros((PAIRS, D_TXT), jnp.float32).at[target].set(values)
    return placed.astype(jnp.bfloat16)


def draw_caption_of(key, part):
    return pair_order(key)


def shard_levels(stream_key, dims, cuts, smallest, largest):
    def one(axis_at, blocks):
        heights = jax.random.uniform(jax.random.fold_in(jax.random.fold_in(stream_key, 6), axis_at), (blocks,), jnp.float32, smallest / len(cuts), largest / len(cuts))
        return jnp.repeat(jnp.exp(heights), dims[axis_at] // blocks).reshape((-1,) + (1,) * (len(dims) - axis_at - 1))

    gain = one(*cuts[0])
    for cut in cuts[1:]:
        gain = gain * one(*cut)
    return gain


def normal_values(rng, dims, scale, reach, shards=(), kind=jnp.bfloat16):
    result = scale * jax.random.normal(rng, dims, jnp.float32)
    if shards:
        result = result * shard_levels(rng, dims, shards, -0.22, 0.18)
    return jnp.clip(result, -reach, reach).astype(kind)


def setup_inputs(seed: int = 0, part: int = 0) -> dict:
    arg_keys = jax.random.split(jax.random.key(seed), 8)
    part_splits = jax.random.split(jax.random.fold_in(arg_keys[7], part), 8)
    return {
        "images": draw_images(jax.random.fold_in(jax.random.fold_in(arg_keys[7], part), 71), part),
        "captions": draw_captions(jax.random.fold_in(jax.random.fold_in(arg_keys[7], part), 71), part),
        "caption_of": draw_caption_of(jax.random.fold_in(jax.random.fold_in(arg_keys[7], part), 71), part),
        "image_landmarks": normal_values(arg_keys[3], (IMG_LM, D_IMG), 1.0, 6.0, ((0, 16),)),
        "image_gamma": jnp.clip(jnp.exp(math.log(40.0) - 1.609438 * jax.random.uniform(arg_keys[4], (IMG_LM,), jnp.float32) ** shard_levels(arg_keys[4], (IMG_LM,), ((0, 16),), -0.2, 0.2)), 8.0, 40.0),
        "text_landmarks": normal_values(arg_keys[5], (TXT_LM, D_TXT), 1.0, 6.0, ((0, 16),)),
        "text_gamma": jnp.clip(jnp.exp(math.log(40.0) - 1.609438 * jax.random.uniform(arg_keys[6], (TXT_LM,), jnp.float32) ** shard_levels(arg_keys[6], (TXT_LM,), ((0, 16),), -0.2, 0.2)), 8.0, 40.0),
    }


def unit_rows(values):
    wide = values.astype(jnp.float32)
    return wide * lax.rsqrt(lax.optimization_barrier(jnp.sum(wide * wide, axis=-1, keepdims=True)) + 1e-06)

def features(left, right):
    inner = lax.dot_general(left, right, (((1,), (1,)), ((), ())), preferred_element_type=jnp.float32)
    return jnp.exp(inner).astype(jnp.bfloat16)

def reference(images, captions, caption_of, image_landmarks, image_gamma, text_landmarks, text_gamma):
    rows_index = jnp.arange(PAIRS, dtype=jnp.int32) // BLOCK * BLOCK + caption_of.astype(jnp.int32)
    paired = jnp.take(captions, rows_index, axis=0)
    image_unit = unit_rows(images).astype(jnp.bfloat16)
    caption_unit = unit_rows(paired).astype(jnp.bfloat16)
    image_keys = (unit_rows(image_landmarks) * image_gamma[:, None]).astype(jnp.bfloat16)
    text_keys = (unit_rows(text_landmarks) * text_gamma[:, None]).astype(jnp.bfloat16)
    image_feats = features(image_unit, image_keys)
    text_feats = features(caption_unit, text_keys)
    image_wide = image_feats.astype(jnp.float32)
    text_wide = text_feats.astype(jnp.float32)
    image_mean = lax.optimization_barrier(jnp.mean(image_wide, axis=0))
    text_mean = lax.optimization_barrier(jnp.mean(text_wide, axis=0))
    image_dev = image_wide - image_mean
    text_dev = text_wide - text_mean
    image_var = lax.optimization_barrier(jnp.mean(image_dev * image_dev, axis=0))
    text_var = lax.optimization_barrier(jnp.mean(text_dev * text_dev, axis=0))
    moment = lax.dot_general(image_feats, text_feats, (((0,), (0,)), ((), ())), preferred_element_type=jnp.float32) / PAIRS
    centred = moment - image_mean[:, None] * text_mean[None, :]
    zstat = math.sqrt(PAIRS) * centred * lax.rsqrt(image_var + 1e-06)[:, None] * lax.rsqrt(text_var + 1e-06)[None, :]
    return (zstat, image_mean, text_mean)
```

```python
import functools
import math

import jax
import jax.numpy as jnp
from jax import lax
from jax.experimental import pallas as pl
from jax.experimental.pallas import tpu as pltpu
from jax.sharding import PartitionSpec as P

MESH = pl.DeviceIdType.MESH
EPS = 1e-06


def unit_rows(wide):
    return wide * lax.rsqrt(jnp.sum(wide * wide, axis=-1, keepdims=True) + EPS)


def diagonal(size):
    return lax.broadcasted_iota(jnp.int32, (size, size), 0) == lax.broadcasted_iota(
        jnp.int32, (size, size), 1
    )


def scaled_keys(marks_ref, gamma_ref, keys_ref):
    total = marks_ref.shape[0]
    size = min(128, total)

    def step(at, carry):
        rows = pl.ds(pl.multiple_of(at * size, size), size)
        unit = unit_rows(marks_ref[rows, :].astype(jnp.float32))
        gamma = jnp.sum(
            jnp.where(diagonal(size), gamma_ref[:, rows], 0.0), axis=1, keepdims=True
        )
        keys_ref[rows, :] = (unit * gamma).astype(jnp.bfloat16)
        return carry

    lax.fori_loop(0, total // size, step, 0)


def standard_features(keys, units, mean_ref, start, scale):
    rows, pairs = keys.shape[0], units.shape[0]
    inner = lax.dot_general(
        keys, units, (((1,), (1,)), ((), ())), preferred_element_type=jnp.float32
    )
    feats = jnp.exp(inner).astype(jnp.bfloat16).astype(jnp.float32)
    mean = jnp.sum(feats, axis=1, keepdims=True) * (1.0 / pairs)
    dev = feats - mean
    var = jnp.sum(dev * dev, axis=1, keepdims=True) * (1.0 / pairs)
    size = min(128, rows)
    for at in range(0, rows, size):
        mean_ref[:, start + at : start + at + size] = jnp.sum(
            jnp.where(diagonal(size), mean[at : at + size], 0.0), axis=0, keepdims=True
        )
    return (dev * (lax.rsqrt(var + EPS) * scale)).astype(jnp.bfloat16)


def exchange_kernel(
    dp, lm, split, chunks,
    images_ref, captions_ref, order_ref, marks_hbm, gamma_ref, words_hbm, text_gamma_ref,
    f_hbm, g_hbm, image_mean_ref, text_mean_ref,
    u_all, c_all, f_all, g_all, marks, words, keys, text_keys,
    load_sem, out_sem,
    u_send, u_recv, u_mate_send, u_mate_recv,
    c_send, c_recv, c_mate_send, c_mate_recv,
    right_send, left_send, f_recv, g_send, g_recv,
):
    me, lane = lax.axis_index("dp"), lax.axis_index("landmark")
    block = images_ref.shape[0]
    part = block // split
    own = marks.shape[0]
    text_own = words.shape[0]
    pairs = u_all.shape[0]
    rows_each = own // chunks

    load_marks = pltpu.make_async_copy(marks_hbm, marks, load_sem.at[0])
    load_words = pltpu.make_async_copy(words_hbm, words, load_sem.at[1])
    load_marks.start()
    load_words.start()

    barrier = pltpu.get_barrier_semaphore()
    for k in range(1, dp):
        pl.semaphore_signal(
            barrier, inc=1, device_id={"dp": lax.rem(me + k, dp)}, device_id_type=MESH
        )
    for k in range(1, lm):
        pl.semaphore_signal(
            barrier, inc=1, device_id={"landmark": lax.rem(lane + k, lm)}, device_id_type=MESH
        )

    mine = pl.ds(pl.multiple_of(me * block, block), block)
    u_all[mine, :] = unit_rows(images_ref[...].astype(jnp.float32)).astype(jnp.bfloat16)
    picks = (
        lax.broadcasted_iota(jnp.int32, (block, block), 0) == order_ref[...]
    ).astype(jnp.bfloat16)
    paired = lax.dot_general(
        picks, captions_ref[...], (((0,), (0,)), ((), ())), preferred_element_type=jnp.float32
    )
    c_all[mine, :] = unit_rows(paired).astype(jnp.bfloat16)
    pl.semaphore_wait(barrier, dp - 1 + lm - 1)

    side = lax.rem(lane, split)
    mate = lane + 1 - 2 * side

    def half(shard):
        return pl.ds(pl.multiple_of(shard * block + side * part, part), part)

    def other_half(shard):
        return pl.ds(pl.multiple_of(shard * block + (1 - side) * part, part), part)

    def block_copy(buf, send, recv, k, shard, target):
        return pltpu.make_async_remote_copy(
            src_ref=buf.at[half(shard), :], dst_ref=buf.at[half(shard), :],
            send_sem=send.at[k], recv_sem=recv.at[shard],
            device_id={"dp": target}, device_id_type=MESH,
        )

    def mate_copy(buf, send, recv, k, shard, rows):
        return pltpu.make_async_remote_copy(
            src_ref=buf.at[rows, :], dst_ref=buf.at[rows, :],
            send_sem=send.at[k], recv_sem=recv.at[shard],
            device_id={"landmark": mate}, device_id_type=MESH,
        )

    sends = []
    for buf, send, recv in ((u_all, u_send, u_recv), (c_all, c_send, c_recv)):
        for k in range(1, dp):
            copy = block_copy(buf, send, recv, k - 1, me, lax.rem(me + k, dp))
            copy.start()
            sends.append(copy)

    def collect(buf, send, recv, mate_send, mate_recv):
        for k in range(1, dp):
            shard = lax.rem(me + dp - k, dp)
            block_copy(buf, send, recv, k - 1, shard, me).wait_recv()
            if split > 1:
                copy = mate_copy(buf, mate_send, mate_recv, k - 1, shard, half(shard))
                copy.start()
                sends.append(copy)
        if split > 1:
            for k in range(1, dp):
                shard = lax.rem(me + dp - k, dp)
                mate_copy(
                    buf, mate_send, mate_recv, k - 1, shard, other_half(shard)
                ).wait_recv()

    load_marks.wait()
    scaled_keys(marks, gamma_ref, keys)
    load_words.wait()
    scaled_keys(words, text_gamma_ref, text_keys)

    def f_rows(shard, c):
        return pl.ds(pl.multiple_of(shard * own + c * rows_each, rows_each), rows_each)

    def hop(shard, c, send, target):
        return pltpu.make_async_remote_copy(
            src_ref=f_all.at[f_rows(shard, c), :], dst_ref=f_all.at[f_rows(shard, c), :],
            send_sem=send.at[shard, c], recv_sem=f_recv.at[shard, c],
            device_id={"dp": target}, device_id_type=MESH,
        )

    def to_right(shard, c):
        return hop(shard, c, right_send, jnp.minimum(me + 1, dp - 1))

    def to_left(shard, c):
        return hop(shard, c, left_send, jnp.maximum(me - 1, 0))

    collect(u_all, u_send, u_recv, u_mate_send, u_mate_recv)
    for c in range(chunks):
        at = c * rows_each
        f_all[f_rows(me, c), :] = standard_features(
            keys[at : at + rows_each, :], u_all[...], image_mean_ref, at, 1.0
        )

        @pl.when(me < dp - 1)
        def _():
            to_right(me, c).start()

        @pl.when(me > 0)
        def _():
            to_left(me, c).start()

    collect(c_all, c_send, c_recv, c_mate_send, c_mate_recv)
    text_mine = pl.ds(pl.multiple_of(lane * text_own, text_own), text_own)
    g_all[text_mine, :] = standard_features(
        text_keys[...], c_all[...], text_mean_ref, 0, 1.0 / math.sqrt(pairs)
    )

    def g_copy(k, shard, target):
        rows = pl.ds(pl.multiple_of(shard * text_own, text_own), text_own)
        return pltpu.make_async_remote_copy(
            src_ref=g_all.at[rows, :], dst_ref=g_all.at[rows, :],
            send_sem=g_send.at[k], recv_sem=g_recv.at[shard],
            device_id={"landmark": target}, device_id_type=MESH,
        )

    for k in range(1, lm):
        copy = g_copy(k - 1, lane, lax.rem(lane + k, lm))
        copy.start()
        sends.append(copy)

    for d in range(1, dp):
        for c in range(chunks):

            @pl.when(me - d >= 0)
            def _():
                to_left(me - d, c).wait_recv()

                @pl.when(me < dp - 1)
                def _():
                    to_right(me - d, c).start()

            @pl.when(me + d < dp)
            def _():
                to_right(me + d, c).wait_recv()

                @pl.when(me > 0)
                def _():
                    to_left(me + d, c).start()

    for k in range(1, lm):
        shard = lax.rem(lane + lm - k, lm)
        g_copy(k - 1, shard, lane).wait_recv()

    f_out = pltpu.make_async_copy(f_all, f_hbm, out_sem.at[0])
    g_out = pltpu.make_async_copy(g_all, g_hbm, out_sem.at[1])
    f_out.start()
    g_out.start()
    for copy in sends:
        copy.wait_send()
    for shard in range(dp):
        for c in range(chunks):

            @pl.when(jnp.logical_and(shard <= me, me < dp - 1))
            def _():
                to_right(shard, c).wait_send()

            @pl.when(jnp.logical_and(shard >= me, me > 0))
            def _():
                to_left(shard, c).wait_send()

    f_out.wait()
    g_out.wait()


def product_kernel(f_ref, g_ref, image_mean_in, text_mean_in, z_ref, image_mean_ref, text_mean_ref):
    z_ref[...] = lax.dot_general(
        f_ref[...], g_ref[...], (((1,), (1,)), ((), ())), preferred_element_type=jnp.float32
    )

    @pl.when(pl.program_id(0) == 0)
    def _():
        image_mean_ref[...] = image_mean_in[...]
        text_mean_ref[...] = text_mean_in[...]


def per_device(
    images, captions, caption_of, image_landmarks, image_gamma, text_landmarks, text_gamma
):
    dp, lm = lax.axis_size("dp"), lax.axis_size("landmark")
    block, width = images.shape
    text_width = captions.shape[1]
    own, text_own = image_landmarks.shape[0], text_landmarks.shape[0]
    pairs = block * dp
    split = 2 if lm % 2 == 0 else 1
    chunks = max(1, own // 256)
    bf16, f32 = jnp.bfloat16, jnp.float32
    vmem = pl.BlockSpec(memory_space=pltpu.VMEM)
    hbm = pl.BlockSpec(memory_space=pl.ANY)
    dma = pltpu.SemaphoreType.DMA
    f, g, image_mean, text_mean = pl.pallas_call(
        functools.partial(exchange_kernel, dp, lm, split, chunks),
        out_shape=(
            jax.ShapeDtypeStruct((dp * own, pairs), bf16),
            jax.ShapeDtypeStruct((lm * text_own, pairs), bf16),
            jax.ShapeDtypeStruct((1, own), f32),
            jax.ShapeDtypeStruct((1, text_own), f32),
        ),
        in_specs=[vmem, vmem, vmem, hbm, vmem, hbm, vmem],
        out_specs=(hbm, hbm, vmem, vmem),
        scratch_shapes=[
            pltpu.VMEM((pairs, width), bf16),
            pltpu.VMEM((pairs, text_width), bf16),
            pltpu.VMEM((dp * own, pairs), bf16),
            pltpu.VMEM((lm * text_own, pairs), bf16),
            pltpu.VMEM((own, width), bf16),
            pltpu.VMEM((text_own, text_width), bf16),
            pltpu.VMEM((own, width), bf16),
            pltpu.VMEM((text_own, text_width), bf16),
            dma((2,)),
            dma((2,)),
            dma((dp,)), dma((dp,)), dma((dp,)), dma((dp,)),
            dma((dp,)), dma((dp,)), dma((dp,)), dma((dp,)),
            dma((dp, chunks)), dma((dp, chunks)), dma((dp, chunks)),
            dma((lm,)), dma((lm,)),
        ],
        compiler_params=pltpu.CompilerParams(
            collective_id=0, has_side_effects=True, vmem_limit_bytes=40 * 2**20
        ),
        name="exchange",
    )(
        images, captions, caption_of[None, :], image_landmarks, image_gamma[None, :],
        text_landmarks, text_gamma[None, :],
    )
    rows, columns = dp * own, lm * text_own
    tile = math.gcd(rows, 512)
    zstat, image_mean, text_mean = pl.pallas_call(
        product_kernel,
        grid=(rows // tile,),
        out_shape=(
            jax.ShapeDtypeStruct((rows, columns), f32),
            jax.ShapeDtypeStruct((1, own), f32),
            jax.ShapeDtypeStruct((1, text_own), f32),
        ),
        in_specs=[
            pl.BlockSpec((tile, pairs), lambda i: (i, 0)),
            pl.BlockSpec((columns, pairs), lambda i: (0, 0)),
            pl.BlockSpec((1, own), lambda i: (0, 0)),
            pl.BlockSpec((1, text_own), lambda i: (0, 0)),
        ],
        out_specs=(
            pl.BlockSpec((tile, columns), lambda i: (i, 0)),
            pl.BlockSpec((1, own), lambda i: (0, 0)),
            pl.BlockSpec((1, text_own), lambda i: (0, 0)),
        ),
        compiler_params=pltpu.CompilerParams(vmem_limit_bytes=40 * 2**20),
        name="product",
    )(f, g, image_mean, text_mean)
    return (zstat, image_mean[0], text_mean[0])


def solution(mesh):
    in_specs = (
        P(("groups", "dp"), None),
        P(("groups", "dp"), None),
        P(("groups", "dp")),
        P(("landmark", "dp"), None),
        P(("landmark", "dp")),
        P(("dp", "landmark"), None),
        P(("dp", "landmark")),
    )
    out_specs = (
        P(("groups", "landmark"), "dp"),
        P(("groups", "landmark", "dp")),
        P(("groups", "dp", "landmark")),
    )
    return jax.shard_map(
        per_device, mesh=mesh, in_specs=in_specs, out_specs=out_specs, check_vma=False
    )
```

```python
import functools
import math

import jax
import jax.numpy as jnp
from jax import lax
from jax.experimental import pallas as pl
from jax.experimental.pallas import tpu as pltpu
from jax.sharding import PartitionSpec as P

MESH = pl.DeviceIdType.MESH
EPS = 1e-06


def unit_rows(wide):
    return wide * lax.rsqrt(jnp.sum(wide * wide, axis=-1, keepdims=True) + EPS)


def diagonal(size):
    return lax.broadcasted_iota(jnp.int32, (size, size), 0) == lax.broadcasted_iota(
        jnp.int32, (size, size), 1
    )


def scaled_keys(marks_ref, gamma_ref, keys_ref):
    total = marks_ref.shape[0]
    size = min(128, total)

    def step(at, carry):
        rows = pl.ds(pl.multiple_of(at * size, size), size)
        unit = unit_rows(marks_ref[rows, :].astype(jnp.float32))
        gamma = jnp.sum(
            jnp.where(diagonal(size), gamma_ref[:, rows], 0.0), axis=1, keepdims=True
        )
        keys_ref[rows, :] = (unit * gamma).astype(jnp.bfloat16)
        return carry

    lax.fori_loop(0, total // size, step, 0)


def standard_features(keys, units, mean_ref, start, scale):
    rows, pairs = keys.shape[0], units.shape[0]
    inner = lax.dot_general(
        keys, units, (((1,), (1,)), ((), ())), preferred_element_type=jnp.float32
    )
    feats = jnp.exp(inner).astype(jnp.bfloat16).astype(jnp.float32)
    mean = jnp.sum(feats, axis=1, keepdims=True) * (1.0 / pairs)
    dev = feats - mean
    var = jnp.sum(dev * dev, axis=1, keepdims=True) * (1.0 / pairs)
    size = min(128, rows)
    for at in range(0, rows, size):
        mean_ref[:, start + at : start + at + size] = jnp.sum(
            jnp.where(diagonal(size), mean[at : at + size], 0.0), axis=0, keepdims=True
        )
    return (dev * (lax.rsqrt(var + EPS) * scale)).astype(jnp.bfloat16)


def exchange_kernel(
    dp, lm, split, chunks,
    images_hbm, captions_hbm, order_hbm, marks_hbm, gamma_hbm, words_hbm, text_gamma_hbm,
    f_all, g_all, image_mean_ref, text_mean_ref,
    images_ref, captions_ref, order_ref, marks, gamma_ref, words, text_gamma_ref,
    u_all, c_all, keys, text_keys,
    load_sem,
    u_send, u_recv, u_mate_send, u_mate_recv,
    c_send, c_recv, c_mate_send, c_mate_recv,
    right_send, left_send, f_recv, g_send, g_recv,
):
    me, lane = lax.axis_index("dp"), lax.axis_index("landmark")
    block = images_ref.shape[0]
    part = block // split
    own = marks.shape[0]
    text_own = words.shape[0]
    pairs = u_all.shape[0]
    rows_each = own // chunks

    loads = [
        pltpu.make_async_copy(src, dst, load_sem.at[at])
        for at, (src, dst) in enumerate((
            (images_hbm, images_ref), (marks_hbm, marks), (gamma_hbm, gamma_ref),
            (captions_hbm, captions_ref), (order_hbm, order_ref),
            (words_hbm, words), (text_gamma_hbm, text_gamma_ref),
        ))
    ]
    for load in loads:
        load.start()

    barrier = pltpu.get_barrier_semaphore()
    for k in range(1, dp):
        pl.semaphore_signal(
            barrier, inc=1, device_id={"dp": lax.rem(me + k, dp)}, device_id_type=MESH
        )
    for k in range(1, lm):
        pl.semaphore_signal(
            barrier, inc=1, device_id={"landmark": lax.rem(lane + k, lm)}, device_id_type=MESH
        )

    mine = pl.ds(pl.multiple_of(me * block, block), block)
    loads[0].wait()
    u_all[mine, :] = unit_rows(images_ref[...].astype(jnp.float32)).astype(jnp.bfloat16)
    pl.semaphore_wait(barrier, dp - 1 + lm - 1)

    side = lax.rem(lane, split)
    mate = lane + 1 - 2 * side

    def half(shard):
        return pl.ds(pl.multiple_of(shard * block + side * part, part), part)

    def other_half(shard):
        return pl.ds(pl.multiple_of(shard * block + (1 - side) * part, part), part)

    def block_copy(buf, send, recv, k, shard, target):
        return pltpu.make_async_remote_copy(
            src_ref=buf.at[half(shard), :], dst_ref=buf.at[half(shard), :],
            send_sem=send.at[k], recv_sem=recv.at[shard],
            device_id={"dp": target}, device_id_type=MESH,
        )

    def mate_copy(buf, send, recv, k, shard, rows):
        return pltpu.make_async_remote_copy(
            src_ref=buf.at[rows, :], dst_ref=buf.at[rows, :],
            send_sem=send.at[k], recv_sem=recv.at[shard],
            device_id={"landmark": mate}, device_id_type=MESH,
        )

    sends = []

    def spread(buf, send, recv):
        for k in range(1, dp):
            copy = block_copy(buf, send, recv, k - 1, me, lax.rem(me + k, dp))
            copy.start()
            sends.append(copy)

    spread(u_all, u_send, u_recv)

    def collect(buf, send, recv, mate_send, mate_recv):
        for k in range(1, dp):
            shard = lax.rem(me + dp - k, dp)
            block_copy(buf, send, recv, k - 1, shard, me).wait_recv()
            if split > 1:
                copy = mate_copy(buf, mate_send, mate_recv, k - 1, shard, half(shard))
                copy.start()
                sends.append(copy)
        if split > 1:
            for k in range(1, dp):
                shard = lax.rem(me + dp - k, dp)
                mate_copy(
                    buf, mate_send, mate_recv, k - 1, shard, other_half(shard)
                ).wait_recv()

    loads[1].wait()
    loads[2].wait()
    scaled_keys(marks, gamma_ref, keys)
    loads[3].wait()
    loads[4].wait()
    picks = (
        lax.broadcasted_iota(jnp.int32, (block, block), 0) == order_ref[...]
    ).astype(jnp.bfloat16)
    paired = lax.dot_general(
        picks, captions_ref[...], (((0,), (0,)), ((), ())), preferred_element_type=jnp.float32
    )
    c_all[mine, :] = unit_rows(paired).astype(jnp.bfloat16)

    def f_rows(shard, c):
        return pl.ds(pl.multiple_of(shard * own + c * rows_each, rows_each), rows_each)

    def hop(shard, c, send, target):
        return pltpu.make_async_remote_copy(
            src_ref=f_all.at[f_rows(shard, c), :], dst_ref=f_all.at[f_rows(shard, c), :],
            send_sem=send.at[shard, c], recv_sem=f_recv.at[shard, c],
            device_id={"dp": target}, device_id_type=MESH,
        )

    def to_right(shard, c):
        return hop(shard, c, right_send, jnp.minimum(me + 1, dp - 1))

    def to_left(shard, c):
        return hop(shard, c, left_send, jnp.maximum(me - 1, 0))

    collect(u_all, u_send, u_recv, u_mate_send, u_mate_recv)
    spread(c_all, c_send, c_recv)
    for c in range(chunks):
        at = c * rows_each
        f_all[f_rows(me, c), :] = standard_features(
            keys[at : at + rows_each, :], u_all[...], image_mean_ref, at, 1.0
        )

        @pl.when(me < dp - 1)
        def _():
            to_right(me, c).start()

        @pl.when(me > 0)
        def _():
            to_left(me, c).start()

    loads[5].wait()
    loads[6].wait()
    scaled_keys(words, text_gamma_ref, text_keys)
    collect(c_all, c_send, c_recv, c_mate_send, c_mate_recv)
    text_mine = pl.ds(pl.multiple_of(lane * text_own, text_own), text_own)
    g_all[text_mine, :] = standard_features(
        text_keys[...], c_all[...], text_mean_ref, 0, 1.0 / math.sqrt(pairs)
    )

    def g_copy(k, shard, target):
        rows = pl.ds(pl.multiple_of(shard * text_own, text_own), text_own)
        return pltpu.make_async_remote_copy(
            src_ref=g_all.at[rows, :], dst_ref=g_all.at[rows, :],
            send_sem=g_send.at[k], recv_sem=g_recv.at[shard],
            device_id={"landmark": target}, device_id_type=MESH,
        )

    for k in range(1, lm):
        copy = g_copy(k - 1, lane, lax.rem(lane + k, lm))
        copy.start()
        sends.append(copy)

    for d in range(1, dp):
        for c in range(chunks):

            @pl.when(me - d >= 0)
            def _():
                to_left(me - d, c).wait_recv()

                @pl.when(me < dp - 1)
                def _():
                    to_right(me - d, c).start()

            @pl.when(me + d < dp)
            def _():
                to_right(me + d, c).wait_recv()

                @pl.when(me > 0)
                def _():
                    to_left(me + d, c).start()

    for k in range(1, lm):
        shard = lax.rem(lane + lm - k, lm)
        g_copy(k - 1, shard, lane).wait_recv()

    for copy in sends:
        copy.wait_send()
    for shard in range(dp):
        for c in range(chunks):

            @pl.when(jnp.logical_and(shard <= me, me < dp - 1))
            def _():
                to_right(shard, c).wait_send()

            @pl.when(jnp.logical_and(shard >= me, me > 0))
            def _():
                to_left(shard, c).wait_send()


def product_kernel(
    tile, slots, f_ref, g_ref, image_mean_in, text_mean_in,
    z_hbm, image_mean_ref, text_mean_ref, buf, sem,
):
    steps = f_ref.shape[0] // tile

    def out(at):
        slot = lax.rem(at, slots)
        rows = pl.ds(pl.multiple_of(at * tile, tile), tile)
        return pltpu.make_async_copy(buf.at[slot], z_hbm.at[rows, :], sem.at[slot])

    def step(at, carry):
        @pl.when(at >= slots)
        def _():
            out(at - slots).wait()

        rows = pl.ds(pl.multiple_of(at * tile, tile), tile)
        buf[lax.rem(at, slots)] = lax.dot_general(
            f_ref[rows, :], g_ref[...], (((1,), (1,)), ((), ())),
            preferred_element_type=jnp.float32,
        )
        out(at).start()
        return carry

    lax.fori_loop(0, steps, step, 0)
    image_mean_ref[...] = image_mean_in[...]
    text_mean_ref[...] = text_mean_in[...]
    for at in range(max(0, steps - slots), steps):
        out(jnp.int32(at)).wait()


def per_device(
    images, captions, caption_of, image_landmarks, image_gamma, text_landmarks, text_gamma
):
    dp, lm = lax.axis_size("dp"), lax.axis_size("landmark")
    block, width = images.shape
    text_width = captions.shape[1]
    own, text_own = image_landmarks.shape[0], text_landmarks.shape[0]
    pairs = block * dp
    split = 2 if lm % 2 == 0 else 1
    chunks = max(1, own // 128)
    bf16, f32 = jnp.bfloat16, jnp.float32
    vmem = pl.BlockSpec(memory_space=pltpu.VMEM)
    hbm = pl.BlockSpec(memory_space=pltpu.HBM)
    dma = pltpu.SemaphoreType.DMA
    f, g, image_mean, text_mean = pl.pallas_call(
        functools.partial(exchange_kernel, dp, lm, split, chunks),
        out_shape=(
            jax.ShapeDtypeStruct((dp * own, pairs), bf16),
            jax.ShapeDtypeStruct((lm * text_own, pairs), bf16),
            jax.ShapeDtypeStruct((1, own), f32),
            jax.ShapeDtypeStruct((1, text_own), f32),
        ),
        in_specs=[hbm] * 7,
        out_specs=(vmem, vmem, vmem, vmem),
        scratch_shapes=[
            pltpu.VMEM((block, width), bf16),
            pltpu.VMEM((block, text_width), bf16),
            pltpu.VMEM((1, block), jnp.int32),
            pltpu.VMEM((own, width), bf16),
            pltpu.VMEM((1, own), f32),
            pltpu.VMEM((text_own, text_width), bf16),
            pltpu.VMEM((1, text_own), f32),
            pltpu.VMEM((pairs, width), bf16),
            pltpu.VMEM((pairs, text_width), bf16),
            pltpu.VMEM((own, width), bf16),
            pltpu.VMEM((text_own, text_width), bf16),
            dma((7,)),
            dma((dp,)), dma((dp,)), dma((dp,)), dma((dp,)),
            dma((dp,)), dma((dp,)), dma((dp,)), dma((dp,)),
            dma((dp, chunks)), dma((dp, chunks)), dma((dp, chunks)),
            dma((lm,)), dma((lm,)),
        ],
        compiler_params=pltpu.CompilerParams(
            collective_id=0, has_side_effects=True, vmem_limit_bytes=40 * 2**20
        ),
        name="exchange",
    )(
        *(
            pltpu.with_memory_space_constraint(value, pltpu.HBM)
            for value in (
                images, captions, caption_of[None, :], image_landmarks, image_gamma[None, :],
                text_landmarks, text_gamma[None, :],
            )
        )
    )
    rows, columns = dp * own, lm * text_own
    tile = math.gcd(rows, 256)
    slots = min(4, rows // tile)
    zstat, image_mean, text_mean = pl.pallas_call(
        functools.partial(product_kernel, tile, slots),
        out_shape=(
            jax.ShapeDtypeStruct((rows, columns), f32),
            jax.ShapeDtypeStruct((1, own), f32),
            jax.ShapeDtypeStruct((1, text_own), f32),
        ),
        in_specs=[vmem] * 4,
        out_specs=(hbm, vmem, vmem),
        scratch_shapes=[pltpu.VMEM((slots, tile, columns), f32), dma((slots,))],
        compiler_params=pltpu.CompilerParams(vmem_limit_bytes=40 * 2**20),
        name="product",
    )(f, g, image_mean, text_mean)
    return (zstat, image_mean[0], text_mean[0])


def solution(mesh):
    in_specs = (
        P(("groups", "dp"), None),
        P(("groups", "dp"), None),
        P(("groups", "dp")),
        P(("landmark", "dp"), None),
        P(("landmark", "dp")),
        P(("dp", "landmark"), None),
        P(("dp", "landmark")),
    )
    out_specs = (
        P(("groups", "landmark"), "dp"),
        P(("groups", "landmark", "dp")),
        P(("groups", "dp", "landmark")),
    )
    return jax.shard_map(
        per_device, mesh=mesh, in_specs=in_specs, out_specs=out_specs, check_vma=False
    )
```

```python
import functools
import math

import jax
import jax.numpy as jnp
from jax import lax
from jax.experimental import pallas as pl
from jax.experimental.pallas import tpu as pltpu
from jax.sharding import PartitionSpec as P

MESH = pl.DeviceIdType.MESH
EPS = 1e-06


def unit_rows(wide):
    return wide * lax.rsqrt(jnp.sum(wide * wide, axis=-1, keepdims=True) + EPS)


def diagonal(size):
    return lax.broadcasted_iota(jnp.int32, (size, size), 0) == lax.broadcasted_iota(
        jnp.int32, (size, size), 1
    )


def scaled_keys(marks_ref, gamma_ref, keys_ref):
    total = marks_ref.shape[0]
    size = min(128, total)

    def step(at, carry):
        rows = pl.ds(pl.multiple_of(at * size, size), size)
        unit = unit_rows(marks_ref[rows, :].astype(jnp.float32))
        gamma = jnp.sum(
            jnp.where(diagonal(size), gamma_ref[:, rows], 0.0), axis=1, keepdims=True
        )
        keys_ref[rows, :] = (unit * gamma).astype(jnp.bfloat16)
        return carry

    lax.fori_loop(0, total // size, step, 0)


def standard_features(keys, units, mean_ref, start, scale):
    rows, pairs = keys.shape[0], units.shape[0]
    inner = lax.dot_general(
        keys, units, (((1,), (1,)), ((), ())), preferred_element_type=jnp.float32
    )
    feats = jnp.exp(inner).astype(jnp.bfloat16).astype(jnp.float32)
    mean = jnp.sum(feats, axis=1, keepdims=True) * (1.0 / pairs)
    dev = feats - mean
    var = jnp.sum(dev * dev, axis=1, keepdims=True) * (1.0 / pairs)
    size = min(128, rows)
    for at in range(0, rows, size):
        mean_ref[:, start + at : start + at + size] = jnp.sum(
            jnp.where(diagonal(size), mean[at : at + size], 0.0), axis=0, keepdims=True
        )
    return (dev * (lax.rsqrt(var + EPS) * scale)).astype(jnp.bfloat16)


def exchange_kernel(
    dp, lm, split, chunks,
    images_hbm, captions_hbm, order_hbm, marks_hbm, gamma_hbm, words_hbm, text_gamma_hbm,
    f_all, g_all, image_mean_ref, text_mean_ref,
    images_ref, captions_ref, order_ref, marks, gamma_ref, words, text_gamma_ref,
    u_all, c_all, keys, text_keys,
    load_sem,
    u_send, u_recv, u_mate_send, u_mate_recv,
    c_send, c_recv, c_mate_send, c_mate_recv,
    right_send, left_send, f_recv, g_send, g_recv,
):
    me, lane = lax.axis_index("dp"), lax.axis_index("landmark")
    block = images_ref.shape[0]
    part = block // split
    own = marks.shape[0]
    text_own = words.shape[0]
    pairs = u_all.shape[0]
    rows_each = own // chunks

    loads = [
        pltpu.make_async_copy(src, dst, load_sem.at[at])
        for at, (src, dst) in enumerate((
            (images_hbm, images_ref), (marks_hbm, marks), (gamma_hbm, gamma_ref),
            (captions_hbm, captions_ref), (order_hbm, order_ref),
            (words_hbm, words), (text_gamma_hbm, text_gamma_ref),
        ))
    ]
    for load in loads:
        load.start()

    barrier = pltpu.get_barrier_semaphore()
    for k in range(1, dp):
        pl.semaphore_signal(
            barrier, inc=1, device_id={"dp": lax.rem(me + k, dp)}, device_id_type=MESH
        )
    for k in range(1, lm):
        pl.semaphore_signal(
            barrier, inc=1, device_id={"landmark": lax.rem(lane + k, lm)}, device_id_type=MESH
        )

    mine = pl.ds(pl.multiple_of(me * block, block), block)
    loads[0].wait()
    u_all[mine, :] = unit_rows(images_ref[...].astype(jnp.float32)).astype(jnp.bfloat16)
    pl.semaphore_wait(barrier, dp - 1 + lm - 1)

    side = lax.rem(lane, split)
    mate = lane + 1 - 2 * side

    def half(shard):
        return pl.ds(pl.multiple_of(shard * block + side * part, part), part)

    def other_half(shard):
        return pl.ds(pl.multiple_of(shard * block + (1 - side) * part, part), part)

    def block_copy(buf, send, recv, k, shard, target):
        return pltpu.make_async_remote_copy(
            src_ref=buf.at[half(shard), :], dst_ref=buf.at[half(shard), :],
            send_sem=send.at[k], recv_sem=recv.at[shard],
            device_id={"dp": target}, device_id_type=MESH,
        )

    def mate_copy(buf, send, recv, k, shard, rows):
        return pltpu.make_async_remote_copy(
            src_ref=buf.at[rows, :], dst_ref=buf.at[rows, :],
            send_sem=send.at[k], recv_sem=recv.at[shard],
            device_id={"landmark": mate}, device_id_type=MESH,
        )

    sends = []

    def spread(buf, send, recv):
        for k in range(1, dp):
            copy = block_copy(buf, send, recv, k - 1, me, lax.rem(me + k, dp))
            copy.start()
            sends.append(copy)

    spread(u_all, u_send, u_recv)

    def collect(buf, send, recv, mate_send, mate_recv):
        for k in range(1, dp):
            shard = lax.rem(me + dp - k, dp)
            block_copy(buf, send, recv, k - 1, shard, me).wait_recv()
            if split > 1:
                copy = mate_copy(buf, mate_send, mate_recv, k - 1, shard, half(shard))
                copy.start()
                sends.append(copy)
        if split > 1:
            for k in range(1, dp):
                shard = lax.rem(me + dp - k, dp)
                mate_copy(
                    buf, mate_send, mate_recv, k - 1, shard, other_half(shard)
                ).wait_recv()

    loads[3].wait()
    loads[4].wait()
    picks = (
        lax.broadcasted_iota(jnp.int32, (block, block), 0) == order_ref[...]
    ).astype(jnp.bfloat16)
    paired = lax.dot_general(
        picks, captions_ref[...], (((0,), (0,)), ((), ())), preferred_element_type=jnp.float32
    )
    c_all[mine, :] = unit_rows(paired).astype(jnp.bfloat16)
    spread(c_all, c_send, c_recv)
    loads[1].wait()
    loads[2].wait()
    scaled_keys(marks, gamma_ref, keys)
    def f_rows(shard, c):
        return pl.ds(pl.multiple_of(shard * own + c * rows_each, rows_each), rows_each)

    def hop(shard, c, send, target):
        return pltpu.make_async_remote_copy(
            src_ref=f_all.at[f_rows(shard, c), :], dst_ref=f_all.at[f_rows(shard, c), :],
            send_sem=send.at[shard, c], recv_sem=f_recv.at[shard, c],
            device_id={"dp": target}, device_id_type=MESH,
        )

    def to_right(shard, c):
        return hop(shard, c, right_send, jnp.minimum(me + 1, dp - 1))

    def to_left(shard, c):
        return hop(shard, c, left_send, jnp.maximum(me - 1, 0))

    collect(u_all, u_send, u_recv, u_mate_send, u_mate_recv)
    for c in range(chunks):
        at = c * rows_each
        f_all[f_rows(me, c), :] = standard_features(
            keys[at : at + rows_each, :], u_all[...], image_mean_ref, at, 1.0
        )

        @pl.when(me < dp - 1)
        def _():
            to_right(me, c).start()

        @pl.when(me > 0)
        def _():
            to_left(me, c).start()

    loads[5].wait()
    loads[6].wait()
    scaled_keys(words, text_gamma_ref, text_keys)
    collect(c_all, c_send, c_recv, c_mate_send, c_mate_recv)
    text_mine = pl.ds(pl.multiple_of(lane * text_own, text_own), text_own)
    g_all[text_mine, :] = standard_features(
        text_keys[...], c_all[...], text_mean_ref, 0, 1.0 / math.sqrt(pairs)
    )

    def g_copy(k, shard, target):
        rows = pl.ds(pl.multiple_of(shard * text_own, text_own), text_own)
        return pltpu.make_async_remote_copy(
            src_ref=g_all.at[rows, :], dst_ref=g_all.at[rows, :],
            send_sem=g_send.at[k], recv_sem=g_recv.at[shard],
            device_id={"landmark": target}, device_id_type=MESH,
        )

    for k in range(1, lm):
        copy = g_copy(k - 1, lane, lax.rem(lane + k, lm))
        copy.start()
        sends.append(copy)

    for d in range(1, dp):
        for c in range(chunks):

            @pl.when(me - d >= 0)
            def _():
                to_left(me - d, c).wait_recv()

                @pl.when(me < dp - 1)
                def _():
                    to_right(me - d, c).start()

            @pl.when(me + d < dp)
            def _():
                to_right(me + d, c).wait_recv()

                @pl.when(me > 0)
                def _():
                    to_left(me + d, c).start()

    for k in range(1, lm):
        shard = lax.rem(lane + lm - k, lm)
        g_copy(k - 1, shard, lane).wait_recv()

    for copy in sends:
        copy.wait_send()
    for shard in range(dp):
        for c in range(chunks):

            @pl.when(jnp.logical_and(shard <= me, me < dp - 1))
            def _():
                to_right(shard, c).wait_send()

            @pl.when(jnp.logical_and(shard >= me, me > 0))
            def _():
                to_left(shard, c).wait_send()


def product_kernel(
    tile, slots, f_ref, g_ref, image_mean_in, text_mean_in,
    z_hbm, image_mean_ref, text_mean_ref, buf, sem,
):
    steps = f_ref.shape[0] // tile

    def out(at):
        slot = lax.rem(at, slots)
        rows = pl.ds(pl.multiple_of(at * tile, tile), tile)
        return pltpu.make_async_copy(buf.at[slot], z_hbm.at[rows, :], sem.at[slot])

    def step(at, carry):
        @pl.when(at >= slots)
        def _():
            out(at - slots).wait()

        rows = pl.ds(pl.multiple_of(at * tile, tile), tile)
        buf[lax.rem(at, slots)] = lax.dot_general(
            f_ref[rows, :], g_ref[...], (((1,), (1,)), ((), ())),
            preferred_element_type=jnp.float32,
        )
        out(at).start()
        return carry

    lax.fori_loop(0, steps, step, 0)
    image_mean_ref[...] = image_mean_in[...]
    text_mean_ref[...] = text_mean_in[...]
    for at in range(max(0, steps - slots), steps):
        out(jnp.int32(at)).wait()


def per_device(
    images, captions, caption_of, image_landmarks, image_gamma, text_landmarks, text_gamma
):
    dp, lm = lax.axis_size("dp"), lax.axis_size("landmark")
    block, width = images.shape
    text_width = captions.shape[1]
    own, text_own = image_landmarks.shape[0], text_landmarks.shape[0]
    pairs = block * dp
    split = 2 if lm % 2 == 0 else 1
    chunks = max(1, own // 256)
    bf16, f32 = jnp.bfloat16, jnp.float32
    vmem = pl.BlockSpec(memory_space=pltpu.VMEM)
    hbm = pl.BlockSpec(memory_space=pltpu.HBM)
    dma = pltpu.SemaphoreType.DMA
    f, g, image_mean, text_mean = pl.pallas_call(
        functools.partial(exchange_kernel, dp, lm, split, chunks),
        out_shape=(
            jax.ShapeDtypeStruct((dp * own, pairs), bf16),
            jax.ShapeDtypeStruct((lm * text_own, pairs), bf16),
            jax.ShapeDtypeStruct((1, own), f32),
            jax.ShapeDtypeStruct((1, text_own), f32),
        ),
        in_specs=[hbm] * 7,
        out_specs=(vmem, vmem, vmem, vmem),
        scratch_shapes=[
            pltpu.VMEM((block, width), bf16),
            pltpu.VMEM((block, text_width), bf16),
            pltpu.VMEM((1, block), jnp.int32),
            pltpu.VMEM((own, width), bf16),
            pltpu.VMEM((1, own), f32),
            pltpu.VMEM((text_own, text_width), bf16),
            pltpu.VMEM((1, text_own), f32),
            pltpu.VMEM((pairs, width), bf16),
            pltpu.VMEM((pairs, text_width), bf16),
            pltpu.VMEM((own, width), bf16),
            pltpu.VMEM((text_own, text_width), bf16),
            dma((7,)),
            dma((dp,)), dma((dp,)), dma((dp,)), dma((dp,)),
            dma((dp,)), dma((dp,)), dma((dp,)), dma((dp,)),
            dma((dp, chunks)), dma((dp, chunks)), dma((dp, chunks)),
            dma((lm,)), dma((lm,)),
        ],
        compiler_params=pltpu.CompilerParams(
            collective_id=0, has_side_effects=True, vmem_limit_bytes=40 * 2**20
        ),
        name="exchange",
    )(
        *(
            pltpu.with_memory_space_constraint(value, pltpu.HBM)
            for value in (
                images, captions, caption_of[None, :], image_landmarks, image_gamma[None, :],
                text_landmarks, text_gamma[None, :],
            )
        )
    )
    rows, columns = dp * own, lm * text_own
    tile = math.gcd(rows, 256)
    slots = min(4, rows // tile)
    zstat, image_mean, text_mean = pl.pallas_call(
        functools.partial(product_kernel, tile, slots),
        out_shape=(
            jax.ShapeDtypeStruct((rows, columns), f32),
            jax.ShapeDtypeStruct((1, own), f32),
            jax.ShapeDtypeStruct((1, text_own), f32),
        ),
        in_specs=[vmem] * 4,
        out_specs=(hbm, vmem, vmem),
        scratch_shapes=[pltpu.VMEM((slots, tile, columns), f32), dma((slots,))],
        compiler_params=pltpu.CompilerParams(vmem_limit_bytes=40 * 2**20),
        name="product",
    )(f, g, image_mean, text_mean)
    return (zstat, image_mean[0], text_mean[0])


def solution(mesh):
    in_specs = (
        P(("groups", "dp"), None),
        P(("groups", "dp"), None),
        P(("groups", "dp")),
        P(("landmark", "dp"), None),
        P(("landmark", "dp")),
        P(("dp", "landmark"), None),
        P(("dp", "landmark")),
    )
    out_specs = (
        P(("groups", "landmark"), "dp"),
        P(("groups", "landmark", "dp")),
        P(("groups", "dp", "landmark")),
    )
    return jax.shard_map(
        per_device, mesh=mesh, in_specs=in_specs, out_specs=out_specs, check_vma=False
    )
```
